32 devices in a mesh: grp: 4 (over y, core), blk: 8 (over z, x).
Axes of the slice: x: 2, y: 2, z: 4, core: 2. Of those that a mesh axis runs over, the one named last changes fastest.
Arguments:
- generator: bfloat16 [4, 16384, 2560], P('grp', 'blk'), may hold values from -0.125 to 0.125
- eta_mask: int32 [4, 128, 20], P('grp', 'blk'), may hold values from 0 to 1
- pair_tiles: bfloat16 [4, 8, 20, 128, 128], P('grp', 'blk'), may hold values from -6 to 6
- tile_order: int32 [4, 8, 20], P('grp', 'blk'), may hold values from 0 to 19, each once within a row
- tile_phase: int32 [4, 8, 20], P('grp', 'blk'), may hold values from 0 to 1
- occupation: float32 [4, 2560], P('grp'), may hold values from -1 to 1
- channel_sign: int32 [4, 4], replicated, may hold values from 0 to 1
- swap_perm: int32 [4, 8, 256], P('grp', 'blk'), may hold values from 0 to 255, each once within a row
Outputs:
- result: float32 [4, 16384, 256], P('grp', 'blk')
The draws below stay inside these ranges and needn't reach their ends.
Inputs may be any that keep to these rules, and one draw needn't show every extreme that they name: `tile_order`: each device's list names each of its 20 held tiles once. `swap_perm`: each device's row names each of its 256 columns once.
All inputs are finite; a program needn't handle non-finite values.
Results may differ from the reference program's by a relative error of at most 0.004.
Values may be sent and summed in bfloat16 or wider, within the bound.
A program may use at most 128 MiB of HBM per device.

```python
import jax
import jax.numpy as jnp
from jax import lax

K = 2560
TILE = 128
BAND = 8
ROWS = 2048
R = 16384
KT = 20
CB = 256
N_GRP = 4
N_BLK = 8


def draw_eta_mask(key, part):
    array_shape = (N_GRP, N_BLK * ROWS // TILE, K // TILE)
    levels = jax.random.randint(key, array_shape, 0, N_GRP + 1)
    groups = lax.broadcasted_iota(jnp.int32, array_shape, 0)
    return (levels <= groups).astype(jnp.int32)


def plant(drawn, rng, smallest, top_value):
    index_at = [jax.random.randint(jax.random.fold_in(rng, axis), (), 0, length) for axis, length in enumerate(drawn.shape)]
    longest = drawn.shape.index(max(drawn.shape))
    neighbour = index_at[:longest] + [(index_at[longest] + 1) % drawn.shape[longest]] + index_at[longest + 1:]
    return drawn.at[tuple(index_at)].set(smallest).at[tuple(neighbour)].set(top_value)


def shard_levels(stream_key, dims, pieces, least, high):
    def one(axis_at, parts):
        steps = jax.random.uniform(jax.random.fold_in(jax.random.fold_in(stream_key, 6), axis_at), (parts,), jnp.float32, least / len(pieces), high / len(pieces))
        return jnp.repeat(jnp.exp(steps), dims[axis_at] // parts).reshape((-1,) + (1,) * (len(dims) - axis_at - 1))

    level = one(*pieces[0])
    for cut in pieces[1:]:
        level = level * one(*cut)
    return level


def bell_draw(stream_key, dims, spread, bound, cuts=(), held_as=jnp.bfloat16):
    drawn = jax.random.normal(stream_key, dims, jnp.float32) * spread
    if len(cuts) > 0:
        drawn = shard_levels(stream_key, dims, cuts, -0.22, 0.18) * drawn
    return jnp.clip(drawn, min=-bound, max=bound).astype(held_as)


def setup_inputs(seed: int = 0) -> dict:
    streams_of = jax.random.split(jax.random.key(seed), 9)
    generator = bell_draw(streams_of[0], (N_GRP, R, K), K ** -0.5, 0.125, ((0, 4), (1, 8)))
    eta_mask = draw_eta_mask(jax.random.fold_in(streams_of[8], 71), 0)
    pair_tiles = bell_draw(streams_of[2], (N_GRP, N_BLK, KT, TILE, TILE), 1.0, 6.0, ((0, 4), (1, 8)))
    tile_order = jax.vmap(lambda own: jax.random.permutation(own, KT))(jax.random.split(streams_of[3], N_GRP * N_BLK)).reshape((N_GRP, N_BLK, KT)).astype(jnp.int32)
    tile_phase = plant(jax.random.randint(streams_of[4], (N_GRP, N_BLK, KT), 0, 2), jax.random.fold_in(streams_of[4], 1), 0, 1).astype(jnp.int32)
    occupation = jnp.clip(jax.random.uniform(streams_of[5], (N_GRP, K), jnp.float32, -1.0, 1.0) * shard_levels(streams_of[5], (N_GRP, K), ((0, 4),), -0.4, 0.0), -1.0, 1.0)
    channel_sign = plant(jax.random.randint(streams_of[6], (N_GRP, N_GRP), 0, 2), jax.random.fold_in(streams_of[6], 1), 0, 1).astype(jnp.int32)
    swap_perm = jax.vmap(lambda own: jax.random.permutation(own, CB))(jax.random.split(streams_of[7], N_GRP * N_BLK)).reshape((N_GRP, N_BLK, CB)).astype(jnp.int32)
    return dict(generator=generator, eta_mask=eta_mask, pair_tiles=pair_tiles, tile_order=tile_order, tile_phase=tile_phase, occupation=occupation, channel_sign=channel_sign, swap_perm=swap_perm)


def reference(generator, eta_mask, pair_tiles, tile_order, tile_phase, occupation, channel_sign, swap_perm):
    tile_count = K // TILE
    slot_count = tile_count // N_GRP
    half_band = BAND // 2
    column_share = BAND * TILE // N_GRP
    chosen = jnp.take_along_axis(pair_tiles, tile_order[:, :, :, None, None], axis=2)
    phases = (1 - 2 * tile_phase).astype(jnp.bfloat16)
    outgoing = chosen * phases[:, :, :, None, None]
    outgoing = outgoing.reshape(N_GRP, N_BLK, N_GRP, slot_count, TILE, TILE)
    arrived = jnp.transpose(outgoing, (2, 1, 0, 3, 4, 5)).reshape(N_GRP, N_BLK, K, TILE)
    scaled = (occupation[:, None, :, None] * arrived.astype(jnp.float32)).astype(jnp.bfloat16)
    scaled_flat = scaled.reshape(N_GRP * N_BLK, K, TILE)
    gen_flat = generator.reshape(N_GRP * N_BLK, ROWS // TILE, TILE, tile_count, TILE)
    mask_flat = eta_mask.reshape(N_GRP * N_BLK, ROWS // TILE, tile_count).astype(jnp.bfloat16)

    def one_device(inputs):
        rows_in, mask_in, flat_index = inputs
        group_index = flat_index // N_BLK
        block_index = flat_index % N_BLK
        masked = (rows_in * mask_in[:, None, :, None]).reshape(ROWS, K)
        offsets = jnp.arange(-half_band, half_band, dtype=jnp.int32)
        selected = group_index * N_BLK + (block_index + offsets) % N_BLK
        band_pieces = jnp.take(scaled_flat, selected, axis=0)
        band_matrix = jnp.transpose(band_pieces, (1, 0, 2)).reshape(K, BAND * TILE)
        return jnp.dot(masked, band_matrix, preferred_element_type=jnp.float32).astype(jnp.bfloat16)

    products = lax.map(one_device, (gen_flat, mask_flat, jnp.arange(N_GRP * N_BLK, dtype=jnp.int32)))
    products = products.reshape(N_GRP, N_BLK, ROWS, N_GRP, column_share)
    sign_values = (1 - 2 * channel_sign).astype(jnp.float32)
    results = []
    for dest_group in range(N_GRP):
        summed = jnp.zeros((N_BLK, ROWS, column_share), jnp.float32)
        for source_group in range(N_GRP):
            summed = summed + sign_values[dest_group, source_group] * products[source_group, :, :, dest_group, :].astype(jnp.float32)
        column_order = jnp.broadcast_to(swap_perm[dest_group][:, None, :], summed.shape)
        partner = jnp.take_along_axis(summed, column_order, axis=2)
        results.append(summed - partner)
    return jnp.stack(results, axis=0).reshape(N_GRP, N_BLK * ROWS, column_share)
```

```python
import functools

import jax
import jax.numpy as jnp
from jax import lax
from jax.experimental import pallas as pl
from jax.experimental.pallas import tpu as pltpu
from jax.sharding import PartitionSpec as P

BAND = 8
MESH = pl.DeviceIdType.MESH


def kernel(
    groups, blocks, gen_hbm, mask_ref, tiles_ref, order_ref, phase_ref, occ_ref, sign_ref, perm_ref,
    out_ref,
    eta, outgoing, arrived, band, prod, recv1, send2, recv2, total,
    gen_sem, ex_send, ex_recv, ring_send, ring_recv, p1_send, p1_recv, p2_send, p2_recv,
):
    tile = tiles_ref.shape[-1]
    tile_count = tiles_ref.shape[2]
    rows = eta.shape[0]
    chunk_tiles = tile_count // groups
    chunk = chunk_tiles * tile
    half = BAND // 2
    whole_ring = blocks == BAND
    g = lax.axis_index("grp")
    b = lax.axis_index("blk")
    y, k = g // 2, g % 2
    partner = y * 2 + 1 - k
    across = ((y + 1) % 2) * 2 + k

    if whole_ring:
        here = (b % 2) * (blocks - 1 - b // 2) + (1 - b % 2) * (b // 2)

        def at(pos):
            pos = (pos + 2 * blocks) % blocks
            far = pos // (blocks // 2)
            return far * (2 * (blocks - 1 - pos) + 1) + (1 - far) * 2 * pos
    else:
        here = b

        def at(pos):
            return (pos + 2 * blocks) % blocks

    def chunks_of(direction, step):
        if step < half:
            return range(groups)
        if whole_ring:
            return range(groups // 2) if direction == 0 else range(groups // 2, groups)
        return range(groups) if direction == 0 else range(0)

    neighbours = (at(here + 1), at(here - 1))

    def owner(j):
        return ((y + j // 2) % (groups // 2)) * 2 + (k + j) % 2

    row_blocks = rows // tile

    def load(i):
        r = pl.ds(i * tile, tile)
        return pltpu.make_async_copy(gen_hbm.at[0, r], eta.at[r], gen_sem.at[i])

    for i in range(row_blocks):
        load(i).start()

    barrier = pltpu.get_barrier_semaphore()
    for other in neighbours:
        pl.semaphore_signal(barrier, inc=1, device_id=(g, other), device_id_type=MESH)
    for j in range(1, groups):
        pl.semaphore_signal(barrier, inc=1, device_id=(owner(j), b), device_id_type=MESH)

    def fill(group, slot):
        for s in range(chunk_tiles):
            q = group * chunk_tiles + s
            phase = (1 - 2 * phase_ref[0, 0, q]).astype(jnp.float32)
            picked = tiles_ref[0, 0, order_ref[0, 0, q]].astype(jnp.float32) * phase
            outgoing[slot, pl.ds(s * tile, tile), :] = picked.astype(jnp.bfloat16)

    def exchange(j):
        return pltpu.make_async_remote_copy(
            outgoing.at[j], arrived.at[j], ex_send.at[j], ex_recv.at[j],
            device_id=(owner(j), b), device_id_type=MESH,
        )

    def scale(j, source):
        o = owner(j)
        for s in range(chunk_tiles):
            start = pl.multiple_of(o * chunk + s * tile, tile)
            occ = jnp.broadcast_to(occ_ref[0:1, pl.ds(start, tile)], (tile, tile)).T
            value = source[j, pl.ds(s * tile, tile), :].astype(jnp.float32)
            band[b % BAND, pl.ds(start, tile), :] = (occ * value).astype(jnp.bfloat16)

    def hop(direction, step, j):
        moved = step - 1 if direction == 0 else 1 - step
        block = at(here - moved)
        r = pl.ds(pl.multiple_of(owner(j) * chunk, tile), chunk)
        piece = band.at[block % BAND, r]
        return pltpu.make_async_remote_copy(
            piece, piece, ring_send.at[direction, step, j], ring_recv.at[direction, step, j],
            device_id=(g, neighbours[direction]), device_id_type=MESH,
        )

    def landed(direction, step, j):
        moved = step if direction == 0 else -step
        block = at(here - moved)
        r = pl.ds(pl.multiple_of(owner(j) * chunk, tile), chunk)
        piece = band.at[block % BAND, r]
        return pltpu.make_async_remote_copy(
            piece, piece, ring_send.at[direction, step, j], ring_recv.at[direction, step, j],
            device_id=(g, neighbours[direction]), device_id_type=MESH,
        )

    for j in range(groups):
        fill(owner(j), j)
    scale(0, outgoing)
    pl.semaphore_wait(barrier, groups + 1)
    for j in (2, 3, 1):
        exchange(j).start()
    for direction in range(2):
        hop(direction, 1, 0).start()
    for j in range(1, groups):
        exchange(j).wait_recv()
        scale(j, arrived)
        for direction in range(2):
            hop(direction, 1, j).start()

    for i in range(row_blocks):
        load(i).wait()

    @pl.loop(0, row_blocks)
    def _(i):
        r = pl.ds(pl.multiple_of(i * tile, tile), tile)
        for t in range(tile_count):
            c = pl.ds(t * tile, tile)
            keep = mask_ref[0, i, t].astype(jnp.float32).astype(jnp.bfloat16)
            eta[r, c] = eta[r, c] * keep

    def place(block):
        return (block - b + half + blocks) % blocks

    def to_partner(p):
        return pltpu.make_async_remote_copy(
            prod.at[p], recv1.at[p], p1_send.at[p], p1_recv.at[p],
            device_id=(partner, b), device_id_type=MESH,
        )

    def to_across(h):
        return pltpu.make_async_remote_copy(
            send2.at[h], recv2.at[h], p2_send.at[h], p2_recv.at[h],
            device_id=(across, b), device_id_type=MESH,
        )

    step_rows = 256

    def multiply(pair):
        places = [place(c) for c in pair]
        signs = [(1 - 2 * sign_ref[p // 2, g]).astype(jnp.float32) for p in places]

        @pl.loop(0, rows // step_rows)
        def _(m):
            r = pl.ds(pl.multiple_of(m * step_rows, step_rows), step_rows)
            right = jnp.concatenate([band[c % BAND] for c in pair], axis=1)
            value = jnp.dot(eta[r, :], right, preferred_element_type=jnp.float32)
            for n in range(2):
                part = value[:, n * tile:(n + 1) * tile] * signs[n]
                prod[places[n], r, :] = part.astype(jnp.bfloat16)

        for p in places:
            @pl.when((p // 2) % 2 != k)
            def _():
                to_partner(p).start()
        return places

    def combine(places):
        for p in places:
            h = p % 2

            @pl.when((p // 2) % 2 == k)
            def _():
                to_partner(p).wait_recv()

                @pl.when(p // 4 != y)
                def _():
                    @pl.loop(0, rows // step_rows)
                    def _(m):
                        r = pl.ds(pl.multiple_of(m * step_rows, step_rows), step_rows)
                        both = prod[p, r, :].astype(jnp.float32) + recv1[p, r, :].astype(jnp.float32)
                        send2[h, r, :] = both.astype(jnp.bfloat16)
                    to_across(h).start()

                @pl.when(p // 4 == y)
                def _():
                    @pl.loop(0, rows // step_rows)
                    def _(m):
                        r = pl.ds(pl.multiple_of(m * step_rows, step_rows), step_rows)
                        both = prod[p, r, :].astype(jnp.float32) + recv1[p, r, :].astype(jnp.float32)
                        total[h, r, :] = both

    waiting = []
    for step in range(1, half + 1):
        for j in range(groups):
            for direction in range(2):
                if j in chunks_of(direction, step):
                    landed(direction, step, j).wait_recv()
                    if step < half and j in chunks_of(direction, step + 1):
                        hop(direction, step + 1, j).start()
        if step < half:
            pair = (at(here - step), at(here + step))
        else:
            pair = (b, at(here - step))
        places = multiply(pair)
        for earlier in waiting:
            combine(earlier)
        waiting = [places]
    for earlier in waiting:
        combine(earlier)

    permutation = jnp.broadcast_to(perm_ref[0, 0:1, :], (2 * tile, 2 * tile))
    chosen = lax.broadcasted_iota(jnp.int32, (2 * tile, 2 * tile), 0) == permutation
    swap = jnp.where(chosen, 1.0, 0.0).astype(jnp.bfloat16)
    for h in range(2):
        to_across(h).wait_recv()

    @pl.loop(0, rows // step_rows)
    def _(m):
        r = pl.ds(pl.multiple_of(m * step_rows, step_rows), step_rows)
        summed = jnp.concatenate(
            [total[h, r, :] + recv2[h, r, :].astype(jnp.float32) for h in range(2)], axis=1
        )
        high = summed.astype(jnp.bfloat16)
        low = (summed - high.astype(jnp.float32)).astype(jnp.bfloat16)
        moved = jnp.dot(high, swap, preferred_element_type=jnp.float32) + jnp.dot(
            low, swap, preferred_element_type=jnp.float32
        )
        out_ref[0, r, :] = summed - moved

    for j in range(1, groups):
        exchange(j).wait_send()
    for step in range(1, half + 1):
        for direction in range(2):
            for j in chunks_of(direction, step):
                hop(direction, step, j).wait_send()
    for p in range(BAND):
        @pl.when((p // 2) % 2 != k)
        def _():
            to_partner(p).wait_send()
    for h in range(2):
        to_across(h).wait_send()


def solution(mesh):
    groups, blocks = mesh.shape["grp"], mesh.shape["blk"]

    def shards(
        generator, eta_mask, pair_tiles, tile_order, tile_phase, occupation, channel_sign, swap_perm
    ):
        tile = pair_tiles.shape[-1]
        rows, width = generator.shape[1:]
        columns = BAND * tile // groups
        bf16 = jnp.bfloat16
        vmem = pl.BlockSpec(memory_space=pltpu.VMEM)
        smem = pl.BlockSpec(memory_space=pltpu.SMEM)
        dma = pltpu.SemaphoreType.DMA
        chunk = width // groups
        ring = (2, BAND // 2 + 1, groups)
        return pl.pallas_call(
            functools.partial(kernel, groups, blocks),
            out_shape=jax.ShapeDtypeStruct((1, rows, columns), jnp.float32),
            in_specs=[pl.BlockSpec(memory_space=pl.ANY), smem, vmem, smem, smem, vmem, smem, vmem],
            out_specs=vmem,
            scratch_shapes=[
                pltpu.VMEM((rows, width), bf16),
                pltpu.VMEM((groups, chunk, tile), bf16),
                pltpu.VMEM((groups, chunk, tile), bf16),
                pltpu.VMEM((BAND, width, tile), bf16),
                pltpu.VMEM((BAND, rows, tile), bf16),
                pltpu.VMEM((BAND, rows, tile), bf16),
                pltpu.VMEM((2, rows, tile), bf16),
                pltpu.VMEM((2, rows, tile), bf16),
                pltpu.VMEM((2, rows, tile), jnp.float32),
                dma((rows // tile,)),
                dma((groups,)),
                dma((groups,)),
                dma(ring),
                dma(ring),
                dma((BAND,)),
                dma((BAND,)),
                dma((2,)),
                dma((2,)),
            ],
            compiler_params=pltpu.CompilerParams(
                collective_id=0, has_side_effects=True, vmem_limit_bytes=60 * 1024 * 1024
            ),
        )(generator, eta_mask, pair_tiles, tile_order, tile_phase, occupation, channel_sign, swap_perm)

    return jax.shard_map(
        shards,
        mesh=mesh,
        in_specs=(
            P("grp", "blk", None),
            P("grp", "blk", None),
            P("grp", "blk", None, None, None),
            P("grp", "blk", None),
            P("grp", "blk", None),
            P("grp", None),
            P(),
            P("grp", "blk", None),
        ),
        out_specs=P("grp", "blk", None),
        check_vma=False,
    )
```

```python
import functools

import jax
import jax.numpy as jnp
from jax import lax
from jax.experimental import pallas as pl
from jax.experimental.pallas import tpu as pltpu
from jax.sharding import PartitionSpec as P

BAND = 8
MESH = pl.DeviceIdType.MESH


def kernel(
    groups, blocks, gen_hbm, mask_ref, tiles_ref, order_ref, phase_ref, occ_ref, sign_ref, perm_ref,
    out_ref,
    eta, outgoing, arrived, band, prod, recv1, send2, recv2, total, partial,
    gen_sem, ex_send, ex_recv, ring_send, ring_recv, p1_send, p1_recv, p2_send, p2_recv,
):
    tile = tiles_ref.shape[-1]
    tile_count = tiles_ref.shape[2]
    rows = eta.shape[0]
    chunk_tiles = tile_count // groups
    chunk = chunk_tiles * tile
    half = BAND // 2
    whole_ring = blocks == BAND
    g = lax.axis_index("grp")
    b = lax.axis_index("blk")
    y, k = g // 2, g % 2
    partner = y * 2 + 1 - k
    across = ((y + 1) % 2) * 2 + k

    if whole_ring:
        here = (b % 2) * (blocks - 1 - b // 2) + (1 - b % 2) * (b // 2)

        def at(pos):
            pos = (pos + 2 * blocks) % blocks
            far = pos // (blocks // 2)
            return far * (2 * (blocks - 1 - pos) + 1) + (1 - far) * 2 * pos
    else:
        here = b

        def at(pos):
            return (pos + 2 * blocks) % blocks

    def chunks_of(direction, step):
        if step < half:
            return range(groups)
        if whole_ring:
            return range(direction, groups, 2)
        return range(groups) if direction == 0 else range(0)

    neighbours = (at(here + 1), at(here - 1))

    def owner(j):
        return ((y + j // 2) % (groups // 2)) * 2 + (k + j) % 2

    row_blocks = rows // tile

    def load(i):
        r = pl.ds(i * tile, tile)
        return pltpu.make_async_copy(gen_hbm.at[0, r], eta.at[r], gen_sem.at[i])

    for i in range(row_blocks):
        load(i).start()

    barrier = pltpu.get_barrier_semaphore()
    for other in neighbours:
        pl.semaphore_signal(barrier, inc=1, device_id=(g, other), device_id_type=MESH)
    for j in range(1, groups):
        pl.semaphore_signal(barrier, inc=1, device_id=(owner(j), b), device_id_type=MESH)

    def fill(group, slot):
        for s in range(chunk_tiles):
            q = group * chunk_tiles + s
            phase = (1 - 2 * phase_ref[0, 0, q]).astype(jnp.float32)
            picked = tiles_ref[0, 0, order_ref[0, 0, q]].astype(jnp.float32) * phase
            outgoing[slot, pl.ds(s * tile, tile), :] = picked.astype(jnp.bfloat16)

    def exchange(j):
        return pltpu.make_async_remote_copy(
            outgoing.at[j], arrived.at[j], ex_send.at[j], ex_recv.at[j],
            device_id=(owner(j), b), device_id_type=MESH,
        )

    def scale(j, source):
        o = owner(j)
        for s in range(chunk_tiles):
            start = pl.multiple_of(o * chunk + s * tile, tile)
            occ = jnp.broadcast_to(occ_ref[0:1, pl.ds(start, tile)], (tile, tile)).T
            value = source[j, pl.ds(s * tile, tile), :].astype(jnp.float32)
            band[b % BAND, pl.ds(start, tile), :] = (occ * value).astype(jnp.bfloat16)

    def hop(direction, step, j):
        moved = step - 1 if direction == 0 else 1 - step
        block = at(here - moved)
        r = pl.ds(pl.multiple_of(owner(j) * chunk, tile), chunk)
        piece = band.at[block % BAND, r]
        return pltpu.make_async_remote_copy(
            piece, piece, ring_send.at[direction, step, j], ring_recv.at[direction, step, j],
            device_id=(g, neighbours[direction]), device_id_type=MESH,
        )

    def landed(direction, step, j):
        moved = step if direction == 0 else -step
        block = at(here - moved)
        r = pl.ds(pl.multiple_of(owner(j) * chunk, tile), chunk)
        piece = band.at[block % BAND, r]
        return pltpu.make_async_remote_copy(
            piece, piece, ring_send.at[direction, step, j], ring_recv.at[direction, step, j],
            device_id=(g, neighbours[direction]), device_id_type=MESH,
        )

    fill(owner(0), 0)
    scale(0, outgoing)
    pl.semaphore_wait(barrier, groups + 1)
    for direction in range(2):
        hop(direction, 1, 0).start()
    for j in (2, 3, 1):
        fill(owner(j), j)
        exchange(j).start()

    def mask_rows(first, last):
        for i in range(first, last):
            load(i).wait()

        @pl.loop(first, last)
        def _(i):
            r = pl.ds(pl.multiple_of(i * tile, tile), tile)
            for t in range(tile_count):
                c = pl.ds(t * tile, tile)
                keep = mask_ref[0, i, t].astype(jnp.float32).astype(jnp.bfloat16)
                eta[r, c] = eta[r, c] * keep

    for j in range(1, groups):
        exchange(j).wait_recv()
        scale(j, arrived)
        for direction in range(2):
            hop(direction, 1, j).start()
        if j < groups - 1:
            mask_rows((j - 1) * row_blocks // (groups - 2), j * row_blocks // (groups - 2))

    def place(block):
        return (block - b + half + blocks) % blocks

    slices = row_blocks // 4
    step_rows = rows // slices

    def rows_of(m):
        return pl.ds(pl.multiple_of(m * step_rows, step_rows), step_rows)

    def to_partner(p, m):
        r = rows_of(m)
        return pltpu.make_async_remote_copy(
            prod.at[p, r], recv1.at[p, r], p1_send.at[p, m], p1_recv.at[p, m],
            device_id=(partner, b), device_id_type=MESH,
        )

    def to_across(h, m):
        r = rows_of(m)
        return pltpu.make_async_remote_copy(
            send2.at[h, r], recv2.at[h, r], p2_send.at[h, m], p2_recv.at[h, m],
            device_id=(across, b), device_id_type=MESH,
        )

    def sign(p):
        return (1 - 2 * sign_ref[p // 2, g]).astype(jnp.float32)

    def hand_over(p, m):
        @pl.when((p // 2) % 2 != k)
        def _():
            to_partner(p, m).start()

    def multiply(pair):
        places = [place(c) for c in pair]
        signs = [sign(p) for p in places]

        @pl.loop(0, slices)
        def _(m):
            r = rows_of(m)
            right = jnp.concatenate([band[c % BAND] for c in pair], axis=1)
            value = jnp.dot(eta[r, :], right, preferred_element_type=jnp.float32)
            for n, p in enumerate(places):
                part = value[:, n * tile:(n + 1) * tile] * signs[n]
                prod[p, r, :] = part.astype(jnp.bfloat16)
            for p in places:
                hand_over(p, m)
        return places

    def half_columns(n):
        span = groups // 2 * chunk
        return pl.ds(pl.multiple_of(((y + n) % 2) * span, tile), span)

    def multiply_first(c):
        columns = half_columns(0)

        @pl.loop(0, slices)
        def _(m):
            r = rows_of(m)
            partial[r, :] = jnp.dot(
                eta[r, columns], band[c % BAND, columns, :], preferred_element_type=jnp.float32
            )

    def multiply_rest(c, p, m):
        columns = half_columns(1)
        r = rows_of(m)
        value = partial[r, :] + jnp.dot(
            eta[r, columns], band[c % BAND, columns, :], preferred_element_type=jnp.float32
        )
        prod[p, r, :] = (value * sign(p)).astype(jnp.bfloat16)
        hand_over(p, m)

    def combine_slice(p, m):
        h = p % 2

        @pl.when((p // 2) % 2 == k)
        def _():
            r = rows_of(m)
            to_partner(p, m).wait_recv()
            both = prod[p, r, :].astype(jnp.float32) + recv1[p, r, :].astype(jnp.float32)

            @pl.when(p // 4 != y)
            def _():
                send2[h, r, :] = both.astype(jnp.bfloat16)
                to_across(h, m).start()

            @pl.when(p // 4 == y)
            def _():
                total[h, r, :] = both

    def combine(places):
        for p in places:
            @pl.loop(0, slices)
            def _(m):
                combine_slice(p, m)

    waiting = []
    for step in range(1, half + 1):
        for j in range(groups):
            for direction in range(2):
                if j in chunks_of(direction, step):
                    landed(direction, step, j).wait_recv()
                    if step < half and j in chunks_of(direction, step + 1):
                        hop(direction, step + 1, j).start()
            if j == groups // 2 - 1:
                if step == 1:
                    own = multiply((b,))
                else:
                    for places in waiting:
                        combine(places)
                    waiting = []
                if step == half:
                    multiply_first(at(here - step))
        if step < half:
            pair = (at(here - step), at(here + step))
            waiting.append(multiply(pair))
            if step == 1:
                waiting.insert(0, own)

    last = at(here - half)
    last_place = place(last)
    multiply_rest(last, last_place, 0)

    @pl.loop(1, slices)
    def _(m):
        multiply_rest(last, last_place, m)
        combine_slice(last_place, m - 1)
    combine_slice(last_place, slices - 1)

    permutation = jnp.broadcast_to(perm_ref[0, 0:1, :], (2 * tile, 2 * tile))
    chosen = lax.broadcasted_iota(jnp.int32, (2 * tile, 2 * tile), 0) == permutation
    swap = jnp.where(chosen, 1.0, 0.0).astype(jnp.bfloat16)

    @pl.loop(0, slices)
    def _(m):
        r = rows_of(m)
        for h in range(2):
            to_across(h, m).wait_recv()
        summed = jnp.concatenate(
            [total[h, r, :] + recv2[h, r, :].astype(jnp.float32) for h in range(2)], axis=1
        )
        high = summed.astype(jnp.bfloat16)
        low = (summed - high.astype(jnp.float32)).astype(jnp.bfloat16)
        moved = jnp.dot(high, swap, preferred_element_type=jnp.float32) + jnp.dot(
            low, swap, preferred_element_type=jnp.float32
        )
        out_ref[0, r, :] = summed - moved

    for j in range(1, groups):
        exchange(j).wait_send()
    for step in range(1, half + 1):
        for direction in range(2):
            for j in chunks_of(direction, step):
                hop(direction, step, j).wait_send()
    for p in range(BAND):
        @pl.when((p // 2) % 2 != k)
        def _():
            for m in range(slices):
                to_partner(p, m).wait_send()
    for h in range(2):
        for m in range(slices):
            to_across(h, m).wait_send()


def solution(mesh):
    groups, blocks = mesh.shape["grp"], mesh.shape["blk"]

    def shards(
        generator, eta_mask, pair_tiles, tile_order, tile_phase, occupation, channel_sign, swap_perm
    ):
        tile = pair_tiles.shape[-1]
        rows, width = generator.shape[1:]
        columns = BAND * tile // groups
        bf16 = jnp.bfloat16
        vmem = pl.BlockSpec(memory_space=pltpu.VMEM)
        smem = pl.BlockSpec(memory_space=pltpu.SMEM)
        dma = pltpu.SemaphoreType.DMA
        chunk = width // groups
        slices = rows // tile // 4
        ring = (2, BAND // 2 + 1, groups)
        return pl.pallas_call(
            functools.partial(kernel, groups, blocks),
            out_shape=jax.ShapeDtypeStruct((1, rows, columns), jnp.float32),
            in_specs=[pl.BlockSpec(memory_space=pl.ANY), smem, vmem, smem, smem, vmem, smem, vmem],
            out_specs=vmem,
            scratch_shapes=[
                pltpu.VMEM((rows, width), bf16),
                pltpu.VMEM((groups, chunk, tile), bf16),
                pltpu.VMEM((groups, chunk, tile), bf16),
                pltpu.VMEM((BAND, width, tile), bf16),
                pltpu.VMEM((BAND, rows, tile), bf16),
                pltpu.VMEM((BAND, rows, tile), bf16),
                pltpu.VMEM((2, rows, tile), bf16),
                pltpu.VMEM((2, rows, tile), bf16),
                pltpu.VMEM((2, rows, tile), jnp.float32),
                pltpu.VMEM((rows, tile), jnp.float32),
                dma((rows // tile,)),
                dma((groups,)),
                dma((groups,)),
                dma(ring),
                dma(ring),
                dma((BAND, slices)),
                dma((BAND, slices)),
                dma((2, slices)),
                dma((2, slices)),
            ],
            compiler_params=pltpu.CompilerParams(
                collective_id=0, has_side_effects=True, vmem_limit_bytes=60 * 1024 * 1024
            ),
        )(generator, eta_mask, pair_tiles, tile_order, tile_phase, occupation, channel_sign, swap_perm)

    return jax.shard_map(
        shards,
        mesh=mesh,
        in_specs=(
            P("grp", "blk", None),
            P("grp", "blk", None),
            P("grp", "blk", None, None, None),
            P("grp", "blk", None),
            P("grp", "blk", None),
            P("grp", None),
            P(),
            P("grp", "blk", None),
        ),
        out_specs=P("grp", "blk", None),
        check_vma=False,
    )
```

```python
import functools

import jax
import jax.numpy as jnp
from jax import lax
from jax.experimental import pallas as pl
from jax.experimental.pallas import tpu as pltpu
from jax.sharding import PartitionSpec as P

BAND = 8
MESH = pl.DeviceIdType.MESH


def kernel(
    groups, blocks, gen_hbm, mask_ref, tiles_ref, order_ref, phase_ref, occ_ref, sign_ref,
    total_out, recv2,
    eta, outgoing, arrived, band, prod, recv1, send2, total, partial,
    gen_sem, ex_send, ex_recv, ring_send, ring_recv, p1_send, p1_recv, p2_send, p2_recv, out_sem,
):
    tile = tiles_ref.shape[-1]
    tile_count = tiles_ref.shape[2]
    rows = eta.shape[0]
    chunk_tiles = tile_count // groups
    chunk = chunk_tiles * tile
    half = BAND // 2
    whole_ring = blocks == BAND
    g = lax.axis_index("grp")
    b = lax.axis_index("blk")
    y, k = g // 2, g % 2
    partner = y * 2 + 1 - k
    across = ((y + 1) % 2) * 2 + k

    if whole_ring:
        here = (b % 2) * (blocks - 1 - b // 2) + (1 - b % 2) * (b // 2)

        def at(pos):
            pos = (pos + 2 * blocks) % blocks
            far = pos // (blocks // 2)
            return far * (2 * (blocks - 1 - pos) + 1) + (1 - far) * 2 * pos
    else:
        here = b

        def at(pos):
            return (pos + 2 * blocks) % blocks

    def chunks_of(direction, step):
        if step < half:
            return range(groups)
        if whole_ring:
            return range(direction, groups, 2)
        return range(groups) if direction == 0 else range(0)

    neighbours = (at(here + 1), at(here - 1))

    def owner(j):
        return ((y + j // 2) % (groups // 2)) * 2 + (k + j) % 2

    row_blocks = rows // tile

    def load(i):
        r = pl.ds(i * tile, tile)
        return pltpu.make_async_copy(gen_hbm.at[0, r], eta.at[r], gen_sem.at[i])

    for i in range(row_blocks):
        load(i).start()

    barrier = pltpu.get_barrier_semaphore()
    for other in neighbours:
        pl.semaphore_signal(barrier, inc=1, device_id=(g, other), device_id_type=MESH)
    for j in range(1, groups):
        pl.semaphore_signal(barrier, inc=1, device_id=(owner(j), b), device_id_type=MESH)

    def fill(group, slot):
        for s in range(chunk_tiles):
            q = group * chunk_tiles + s
            phase = (1 - 2 * phase_ref[0, 0, q]).astype(jnp.float32)
            picked = tiles_ref[0, 0, order_ref[0, 0, q]].astype(jnp.float32) * phase
            outgoing[slot, pl.ds(s * tile, tile), :] = picked.astype(jnp.bfloat16)

    def exchange(j):
        return pltpu.make_async_remote_copy(
            outgoing.at[j], arrived.at[j], ex_send.at[j], ex_recv.at[j],
            device_id=(owner(j), b), device_id_type=MESH,
        )

    def scale(j, source):
        o = owner(j)
        for s in range(chunk_tiles):
            start = pl.multiple_of(o * chunk + s * tile, tile)
            occ = jnp.broadcast_to(occ_ref[0:1, pl.ds(start, tile)], (tile, tile)).T
            value = source[j, pl.ds(s * tile, tile), :].astype(jnp.float32)
            band[b % BAND, pl.ds(start, tile), :] = (occ * value).astype(jnp.bfloat16)

    def hop(direction, step, j):
        moved = step - 1 if direction == 0 else 1 - step
        block = at(here - moved)
        r = pl.ds(pl.multiple_of(owner(j) * chunk, tile), chunk)
        piece = band.at[block % BAND, r]
        return pltpu.make_async_remote_copy(
            piece, piece, ring_send.at[direction, step, j], ring_recv.at[direction, step, j],
            device_id=(g, neighbours[direction]), device_id_type=MESH,
        )

    def landed(direction, step, j):
        moved = step if direction == 0 else -step
        block = at(here - moved)
        r = pl.ds(pl.multiple_of(owner(j) * chunk, tile), chunk)
        piece = band.at[block % BAND, r]
        return pltpu.make_async_remote_copy(
            piece, piece, ring_send.at[direction, step, j], ring_recv.at[direction, step, j],
            device_id=(g, neighbours[direction]), device_id_type=MESH,
        )

    fill(owner(0), 0)
    scale(0, outgoing)
    pl.semaphore_wait(barrier, groups + 1)
    for direction in range(2):
        hop(direction, 1, 0).start()
    for j in (2, 3, 1):
        fill(owner(j), j)
        exchange(j).start()

    def mask_rows(first, last):
        for i in range(first, last):
            load(i).wait()

        @pl.loop(first, last)
        def _(i):
            r = pl.ds(pl.multiple_of(i * tile, tile), tile)
            for t in range(tile_count):
                c = pl.ds(t * tile, tile)
                keep = mask_ref[0, i, t].astype(jnp.float32).astype(jnp.bfloat16)
                eta[r, c] = eta[r, c] * keep

    for j in range(1, groups):
        exchange(j).wait_recv()
        scale(j, arrived)
        for direction in range(2):
            hop(direction, 1, j).start()
        if j < groups - 1:
            mask_rows((j - 1) * row_blocks // (groups - 2), j * row_blocks // (groups - 2))

    def place(block):
        return (block - b + half + blocks) % blocks

    slices = row_blocks // 4
    step_rows = rows // slices

    def rows_of(m):
        return pl.ds(pl.multiple_of(m * step_rows, step_rows), step_rows)

    def to_partner(p, m):
        r = rows_of(m)
        return pltpu.make_async_remote_copy(
            prod.at[p, r], recv1.at[p, r], p1_send.at[p, m], p1_recv.at[p, m],
            device_id=(partner, b), device_id_type=MESH,
        )

    def to_across(h, m):
        r = rows_of(m)
        return pltpu.make_async_remote_copy(
            send2.at[h, r], recv2.at[h, r], p2_send.at[h, m], p2_recv.at[h, m],
            device_id=(across, b), device_id_type=MESH,
        )

    def keep_total(h, m):
        r = rows_of(m)
        return pltpu.make_async_copy(total.at[h, r], total_out.at[h, r], out_sem.at[h, m])

    def sign(p):
        return (1 - 2 * sign_ref[p // 2, g]).astype(jnp.float32)

    def hand_over(p, m):
        @pl.when((p // 2) % 2 != k)
        def _():
            to_partner(p, m).start()

    def multiply(pair):
        places = [place(c) for c in pair]
        signs = [sign(p) for p in places]

        @pl.loop(0, slices)
        def _(m):
            r = rows_of(m)
            right = jnp.concatenate([band[c % BAND] for c in pair], axis=1)
            value = jnp.dot(eta[r, :], right, preferred_element_type=jnp.float32)
            for n, p in enumerate(places):
                part = value[:, n * tile:(n + 1) * tile] * signs[n]
                prod[p, r, :] = part.astype(jnp.bfloat16)
            for p in places:
                hand_over(p, m)
        return places

    def half_columns(n):
        span = groups // 2 * chunk
        return pl.ds(pl.multiple_of(((y + n) % 2) * span, tile), span)

    def right_of(pair, columns):
        pieces = [band[c % BAND, columns, :] for c in pair]
        return pieces[0] if len(pieces) == 1 else jnp.concatenate(pieces, axis=1)

    def multiply_first(pair):
        columns = half_columns(0)

        @pl.loop(0, slices)
        def _(m):
            r = rows_of(m)
            partial[r, pl.ds(0, len(pair) * tile)] = jnp.dot(
                eta[r, columns], right_of(pair, columns), preferred_element_type=jnp.float32
            )

    def multiply_rest(pair):
        columns = half_columns(1)
        places = [place(c) for c in pair]
        lag = 2

        @pl.loop(0, slices + lag)
        def _(m):
            @pl.when(m < slices)
            def _():
                r = rows_of(m)
                value = partial[r, pl.ds(0, len(pair) * tile)] + jnp.dot(
                    eta[r, columns], right_of(pair, columns), preferred_element_type=jnp.float32
                )
                for n, p in enumerate(places):
                    part = value[:, n * tile:(n + 1) * tile] * sign(p)
                    prod[p, r, :] = part.astype(jnp.bfloat16)
                for p in places:
                    hand_over(p, m)

            @pl.when(m >= lag)
            def _():
                for p in places:
                    combine_slice(p, m - lag)

    def combine_slice(p, m):
        h = p % 2

        @pl.when((p // 2) % 2 == k)
        def _():
            r = rows_of(m)
            to_partner(p, m).wait_recv()
            both = prod[p, r, :].astype(jnp.float32) + recv1[p, r, :].astype(jnp.float32)

            @pl.when(p // 4 != y)
            def _():
                send2[h, r, :] = both.astype(jnp.bfloat16)
                to_across(h, m).start()

            @pl.when(p // 4 == y)
            def _():
                total[h, r, :] = both
                keep_total(h, m).start()

    def combine(places):
        for p in places:
            @pl.loop(0, slices)
            def _(m):
                combine_slice(p, m)

    waiting = []
    for step in range(1, half + 1):
        for j in range(groups):
            for direction in range(2):
                if j in chunks_of(direction, step):
                    landed(direction, step, j).wait_recv()
                    if step < half and j in chunks_of(direction, step + 1):
                        hop(direction, step + 1, j).start()
            if j == groups // 2 - 1:
                if step == 1:
                    own = multiply((b,))
                else:
                    for places in waiting:
                        combine(places)
                    waiting = []
                if step == half - 1:
                    multiply_first((at(here - step), at(here + step)))
                if step == half:
                    multiply_first((at(here - step),))
        if step < half - 1:
            pair = (at(here - step), at(here + step))
            waiting.append(multiply(pair))
            if step == 1:
                waiting.insert(0, own)
        elif step == half - 1:
            multiply_rest((at(here - step), at(here + step)))
        else:
            multiply_rest((at(here - step),))

    for h in range(2):
        for m in range(slices):
            keep_total(h, m).wait()
            to_across(h, m).wait_recv()

    for j in range(1, groups):
        exchange(j).wait_send()
    for step in range(1, half + 1):
        for direction in range(2):
            for j in chunks_of(direction, step):
                hop(direction, step, j).wait_send()
    for p in range(BAND):
        @pl.when((p // 2) % 2 != k)
        def _():
            for m in range(slices):
                to_partner(p, m).wait_send()
    for h in range(2):
        for m in range(slices):
            to_across(h, m).wait_send()


def exchange_kernel(total_ref, other_ref, perm_ref, out_ref):
    tile = total_ref.shape[2]
    permutation = jnp.broadcast_to(perm_ref[0, 0:1, :], (2 * tile, 2 * tile))
    chosen = lax.broadcasted_iota(jnp.int32, (2 * tile, 2 * tile), 0) == permutation
    swap = jnp.where(chosen, 1.0, 0.0).astype(jnp.bfloat16)
    summed = jnp.concatenate(
        [total_ref[h] + other_ref[h].astype(jnp.float32) for h in range(2)], axis=1
    )
    high = summed.astype(jnp.bfloat16)
    low = (summed - high.astype(jnp.float32)).astype(jnp.bfloat16)
    moved = jnp.dot(high, swap, preferred_element_type=jnp.float32) + jnp.dot(
        low, swap, preferred_element_type=jnp.float32
    )
    out_ref[0] = summed - moved


def solution(mesh):
    groups, blocks = mesh.shape["grp"], mesh.shape["blk"]

    def shards(
        generator, eta_mask, pair_tiles, tile_order, tile_phase, occupation, channel_sign, swap_perm
    ):
        tile = pair_tiles.shape[-1]
        rows, width = generator.shape[1:]
        columns = BAND * tile // groups
        bf16 = jnp.bfloat16
        vmem = pl.BlockSpec(memory_space=pltpu.VMEM)
        smem = pl.BlockSpec(memory_space=pltpu.SMEM)
        dma = pltpu.SemaphoreType.DMA
        chunk = width // groups
        slices = rows // tile // 4
        ring = (2, BAND // 2 + 1, groups)
        total, other = pl.pallas_call(
            functools.partial(kernel, groups, blocks),
            out_shape=(
                jax.ShapeDtypeStruct((2, rows, tile), jnp.float32),
                jax.ShapeDtypeStruct((2, rows, tile), bf16),
            ),
            in_specs=[pl.BlockSpec(memory_space=pl.ANY), smem, vmem, smem, smem, vmem, smem],
            out_specs=(pl.BlockSpec(memory_space=pl.ANY), pl.BlockSpec(memory_space=pl.ANY)),
            scratch_shapes=[
                pltpu.VMEM((rows, width), bf16),
                pltpu.VMEM((groups, chunk, tile), bf16),
                pltpu.VMEM((groups, chunk, tile), bf16),
                pltpu.VMEM((BAND, width, tile), bf16),
                pltpu.VMEM((BAND, rows, tile), bf16),
                pltpu.VMEM((BAND, rows, tile), bf16),
                pltpu.VMEM((2, rows, tile), bf16),
                pltpu.VMEM((2, rows, tile), jnp.float32),
                pltpu.VMEM((rows, 2 * tile), jnp.float32),
                dma((rows // tile,)),
                dma((groups,)),
                dma((groups,)),
                dma(ring),
                dma(ring),
                dma((BAND, slices)),
                dma((BAND, slices)),
                dma((2, slices)),
                dma((2, slices)),
                dma((2, slices)),
            ],
            compiler_params=pltpu.CompilerParams(
                collective_id=0, has_side_effects=True, vmem_limit_bytes=60 * 1024 * 1024
            ),
        )(generator, eta_mask, pair_tiles, tile_order, tile_phase, occupation, channel_sign)
        step = rows // slices
        part = pl.BlockSpec((2, step, tile), lambda m: (0, m, 0))
        return pl.pallas_call(
            exchange_kernel,
            grid=(slices,),
            out_shape=jax.ShapeDtypeStruct((1, rows, columns), jnp.float32),
            in_specs=[part, part, pl.BlockSpec((1, 1, columns), lambda m: (0, 0, 0))],
            out_specs=pl.BlockSpec((1, step, columns), lambda m: (0, m, 0)),
        )(total, other, swap_perm)

    return jax.shard_map(
        shards,
        mesh=mesh,
        in_specs=(
            P("grp", "blk", None),
            P("grp", "blk", None),
            P("grp", "blk", None, None, None),
            P("grp", "blk", None),
            P("grp", "blk", None),
            P("grp", None),
            P(),
            P("grp", "blk", None),
        ),
        out_specs=P("grp", "blk", None),
        check_vma=False,
    )
```

```python
import functools

import jax
import jax.numpy as jnp
from jax import lax
from jax.experimental import pallas as pl
from jax.experimental.pallas import tpu as pltpu
from jax.sharding import PartitionSpec as P

BAND = 8
MESH = pl.DeviceIdType.MESH


def kernel(
    groups, blocks, gen_hbm, mask_ref, tiles_ref, order_ref, phase_ref, occ_ref, sign_ref,
    total_out, recv2,
    eta, outgoing, arrived, band, prod, recv1, send2, total, partial,
    gen_sem, ex_send, ex_recv, ring_send, ring_recv, p1_send, p1_recv, p2_send, p2_recv, out_sem,
):
    tile = tiles_ref.shape[-1]
    tile_count = tiles_ref.shape[2]
    rows = eta.shape[0]
    chunk_tiles = tile_count // groups
    chunk = chunk_tiles * tile
    half = BAND // 2
    whole_ring = blocks == BAND
    g = lax.axis_index("grp")
    b = lax.axis_index("blk")
    y, k = g // 2, g % 2
    partner = y * 2 + 1 - k
    across = ((y + 1) % 2) * 2 + k

    if whole_ring:
        here = (b % 2) * (blocks - 1 - b // 2) + (1 - b % 2) * (b // 2)

        def at(pos):
            pos = (pos + 2 * blocks) % blocks
            far = pos // (blocks // 2)
            return far * (2 * (blocks - 1 - pos) + 1) + (1 - far) * 2 * pos
    else:
        here = b

        def at(pos):
            return (pos + 2 * blocks) % blocks

    def chunks_of(direction, step):
        if step < half:
            return range(groups)
        if whole_ring:
            return range(direction, groups, 2)
        return range(groups) if direction == 0 else range(0)

    neighbours = (at(here + 1), at(here - 1))

    def owner(j):
        return ((y + j // 2) % (groups // 2)) * 2 + (k + j) % 2

    row_blocks = rows // tile

    def load(i):
        r = pl.ds(i * tile, tile)
        return pltpu.make_async_copy(gen_hbm.at[0, r], eta.at[r], gen_sem.at[i])

    for i in range(row_blocks):
        load(i).start()

    barrier = pltpu.get_barrier_semaphore()
    for other in neighbours:
        pl.semaphore_signal(barrier, inc=1, device_id=(g, other), device_id_type=MESH)
    for j in range(1, groups):
        pl.semaphore_signal(barrier, inc=1, device_id=(owner(j), b), device_id_type=MESH)

    def fill(group, slot):
        for s in range(chunk_tiles):
            q = group * chunk_tiles + s
            phase = (1 - 2 * phase_ref[0, 0, q]).astype(jnp.float32)
            picked = tiles_ref[0, 0, order_ref[0, 0, q]].astype(jnp.float32) * phase
            outgoing[slot, pl.ds(s * tile, tile), :] = picked.astype(jnp.bfloat16)

    def exchange(j):
        return pltpu.make_async_remote_copy(
            outgoing.at[j], arrived.at[j], ex_send.at[j], ex_recv.at[j],
            device_id=(owner(j), b), device_id_type=MESH,
        )

    def scale(j, source):
        o = owner(j)
        for s in range(chunk_tiles):
            start = pl.multiple_of(o * chunk + s * tile, tile)
            occ = jnp.broadcast_to(occ_ref[0:1, pl.ds(start, tile)], (tile, tile)).T
            value = source[j, pl.ds(s * tile, tile), :].astype(jnp.float32)
            band[b % BAND, pl.ds(start, tile), :] = (occ * value).astype(jnp.bfloat16)

    def hop(direction, step, j):
        moved = step - 1 if direction == 0 else 1 - step
        block = at(here - moved)
        r = pl.ds(pl.multiple_of(owner(j) * chunk, tile), chunk)
        piece = band.at[block % BAND, r]
        return pltpu.make_async_remote_copy(
            piece, piece, ring_send.at[direction, step, j], ring_recv.at[direction, step, j],
            device_id=(g, neighbours[direction]), device_id_type=MESH,
        )

    def landed(direction, step, j):
        moved = step if direction == 0 else -step
        block = at(here - moved)
        r = pl.ds(pl.multiple_of(owner(j) * chunk, tile), chunk)
        piece = band.at[block % BAND, r]
        return pltpu.make_async_remote_copy(
            piece, piece, ring_send.at[direction, step, j], ring_recv.at[direction, step, j],
            device_id=(g, neighbours[direction]), device_id_type=MESH,
        )

    fill(owner(0), 0)
    scale(0, outgoing)
    pl.semaphore_wait(barrier, groups + 1)
    for direction in range(2):
        hop(direction, 1, 0).start()
    for j in (2, 3, 1):
        fill(owner(j), j)
        exchange(j).start()

    def mask_rows(first, last):
        for i in range(first, last):
            load(i).wait()

        @pl.loop(first, last)
        def _(i):
            r = pl.ds(pl.multiple_of(i * tile, tile), tile)
            for t in range(tile_count):
                c = pl.ds(t * tile, tile)
                keep = mask_ref[0, i, t].astype(jnp.float32).astype(jnp.bfloat16)
                eta[r, c] = eta[r, c] * keep

    for j in range(1, groups):
        exchange(j).wait_recv()
        scale(j, arrived)
        for direction in range(2):
            hop(direction, 1, j).start()
        if j < groups - 1:
            mask_rows((j - 1) * row_blocks // (groups - 2), j * row_blocks // (groups - 2))

    def place(block):
        return (block - b + half + blocks) % blocks

    slices = row_blocks // 4
    step_rows = rows // slices

    def rows_of(m):
        return pl.ds(pl.multiple_of(m * step_rows, step_rows), step_rows)

    def to_partner(p, m):
        r = rows_of(m)
        return pltpu.make_async_remote_copy(
            prod.at[p, r], recv1.at[p, r], p1_send.at[p, m], p1_recv.at[p, m],
            device_id=(partner, b), device_id_type=MESH,
        )

    def to_across(h, m):
        r = rows_of(m)
        return pltpu.make_async_remote_copy(
            send2.at[h, r], recv2.at[h, r], p2_send.at[h, m], p2_recv.at[h, m],
            device_id=(across, b), device_id_type=MESH,
        )

    def keep_total(h, m):
        r = rows_of(m)
        return pltpu.make_async_copy(total.at[h, r], total_out.at[h, r], out_sem.at[h, m])

    def sign(p):
        return (1 - 2 * sign_ref[p // 2, g]).astype(jnp.float32)

    def hand_over(p, m):
        @pl.when((p // 2) % 2 != k)
        def _():
            to_partner(p, m).start()

    def multiply(pair):
        places = [place(c) for c in pair]
        signs = [sign(p) for p in places]

        @pl.loop(0, slices)
        def _(m):
            r = rows_of(m)
            right = jnp.concatenate([band[c % BAND] for c in pair], axis=1)
            value = jnp.dot(eta[r, :], right, preferred_element_type=jnp.float32)
            for n, p in enumerate(places):
                part = value[:, n * tile:(n + 1) * tile] * signs[n]
                prod[p, r, :] = part.astype(jnp.bfloat16)
            for p in places:
                hand_over(p, m)
        return places

    def half_columns(n):
        span = groups // 2 * chunk
        return pl.ds(pl.multiple_of(((y + n) % 2) * span, tile), span)

    def right_of(pair, columns):
        pieces = [band[c % BAND, columns, :] for c in pair]
        return pieces[0] if len(pieces) == 1 else jnp.concatenate(pieces, axis=1)

    def multiply_first(pair):
        columns = half_columns(0)

        @pl.loop(0, slices)
        def _(m):
            r = rows_of(m)
            partial[r, pl.ds(0, len(pair) * tile)] = jnp.dot(
                eta[r, columns], right_of(pair, columns), preferred_element_type=jnp.float32
            )

    def multiply_rest(pair):
        columns = half_columns(1)
        places = [place(c) for c in pair]
        lag = 2

        @pl.loop(0, slices + lag)
        def _(m):
            @pl.when(m < slices)
            def _():
                r = rows_of(m)
                value = partial[r, pl.ds(0, len(pair) * tile)] + jnp.dot(
                    eta[r, columns], right_of(pair, columns), preferred_element_type=jnp.float32
                )
                for n, p in enumerate(places):
                    part = value[:, n * tile:(n + 1) * tile] * sign(p)
                    prod[p, r, :] = part.astype(jnp.bfloat16)
                for p in places:
                    hand_over(p, m)

            @pl.when(m >= lag)
            def _():
                for p in places:
                    combine_slice(p, m - lag)

    def combine_slice(p, m):
        h = p % 2

        @pl.when((p // 2) % 2 == k)
        def _():
            r = rows_of(m)
            to_partner(p, m).wait_recv()
            both = prod[p, r, :].astype(jnp.float32) + recv1[p, r, :].astype(jnp.float32)

            @pl.when(p // 4 != y)
            def _():
                send2[h, r, :] = both.astype(jnp.bfloat16)
                to_across(h, m).start()

            @pl.when(p // 4 == y)
            def _():
                total[h, r, :] = both
                keep_total(h, m).start()

    def combine(places):
        for p in places:
            @pl.loop(0, slices)
            def _(m):
                combine_slice(p, m)

    waiting = []
    for step in range(1, half + 1):
        for j in range(groups):
            for direction in range(2):
                if j in chunks_of(direction, step):
                    landed(direction, step, j).wait_recv()
                    if step < half and j in chunks_of(direction, step + 1):
                        hop(direction, step + 1, j).start()
            if j == groups // 2 - 1:
                if step == 1:
                    own = multiply((b,))
                else:
                    for places in waiting:
                        combine(places)
                    waiting = []
                if step == half - 1:
                    multiply_first((at(here - step), at(here + step)))
                if step == half:
                    multiply_first((at(here - step),))
        if step < half - 1:
            pair = (at(here - step), at(here + step))
            waiting.append(multiply(pair))
            if step == 1:
                waiting.insert(0, own)
        elif step == half - 1:
            multiply_rest((at(here - step), at(here + step)))
        else:
            multiply_rest((at(here - step),))

    for h in range(2):
        for m in range(slices):
            keep_total(h, m).wait()
            to_across(h, m).wait_recv()

    for j in range(1, groups):
        exchange(j).wait_send()
    for step in range(1, half + 1):
        for direction in range(2):
            for j in chunks_of(direction, step):
                hop(direction, step, j).wait_send()
    for p in range(BAND):
        @pl.when((p // 2) % 2 != k)
        def _():
            for m in range(slices):
                to_partner(p, m).wait_send()
    for h in range(2):
        for m in range(slices):
            to_across(h, m).wait_send()


def exchange_kernel(total_ref, other_ref, perm_ref, out_ref):
    tile = total_ref.shape[2]
    step = out_ref.shape[1]
    r = pl.ds(pl.multiple_of(pl.program_id(0) * step, step), step)
    permutation = jnp.broadcast_to(perm_ref[0, 0:1, :], (2 * tile, 2 * tile))
    chosen = lax.broadcasted_iota(jnp.int32, (2 * tile, 2 * tile), 0) == permutation
    swap = jnp.where(chosen, 1.0, 0.0).astype(jnp.bfloat16)
    summed = jnp.concatenate(
        [total_ref[h, r, :] + other_ref[h, r, :].astype(jnp.float32) for h in range(2)], axis=1
    )
    high = summed.astype(jnp.bfloat16)
    low = (summed - high.astype(jnp.float32)).astype(jnp.bfloat16)
    moved = jnp.dot(high, swap, preferred_element_type=jnp.float32) + jnp.dot(
        low, swap, preferred_element_type=jnp.float32
    )
    out_ref[0] = summed - moved


def solution(mesh):
    groups, blocks = mesh.shape["grp"], mesh.shape["blk"]

    def shards(
        generator, eta_mask, pair_tiles, tile_order, tile_phase, occupation, channel_sign, swap_perm
    ):
        tile = pair_tiles.shape[-1]
        rows, width = generator.shape[1:]
        columns = BAND * tile // groups
        bf16 = jnp.bfloat16
        vmem = pl.BlockSpec(memory_space=pltpu.VMEM)
        smem = pl.BlockSpec(memory_space=pltpu.SMEM)
        dma = pltpu.SemaphoreType.DMA
        chunk = width // groups
        slices = rows // tile // 4
        ring = (2, BAND // 2 + 1, groups)
        total, other = pl.pallas_call(
            functools.partial(kernel, groups, blocks),
            out_shape=(
                jax.ShapeDtypeStruct((2, rows, tile), jnp.float32),
                jax.ShapeDtypeStruct((2, rows, tile), bf16),
            ),
            in_specs=[pl.BlockSpec(memory_space=pl.ANY), smem, vmem, smem, smem, vmem, smem],
            out_specs=(pl.BlockSpec(memory_space=pl.ANY), pl.BlockSpec(memory_space=pl.ANY)),
            scratch_shapes=[
                pltpu.VMEM((rows, width), bf16),
                pltpu.VMEM((groups, chunk, tile), bf16),
                pltpu.VMEM((groups, chunk, tile), bf16),
                pltpu.VMEM((BAND, width, tile), bf16),
                pltpu.VMEM((BAND, rows, tile), bf16),
                pltpu.VMEM((BAND, rows, tile), bf16),
                pltpu.VMEM((2, rows, tile), bf16),
                pltpu.VMEM((2, rows, tile), jnp.float32),
                pltpu.VMEM((rows, 2 * tile), jnp.float32),
                dma((rows // tile,)),
                dma((groups,)),
                dma((groups,)),
                dma(ring),
                dma(ring),
                dma((BAND, slices)),
                dma((BAND, slices)),
                dma((2, slices)),
                dma((2, slices)),
                dma((2, slices)),
            ],
            compiler_params=pltpu.CompilerParams(
                collective_id=0, has_side_effects=True, vmem_limit_bytes=50 * 1024 * 1024
            ),
        )(generator, eta_mask, pair_tiles, tile_order, tile_phase, occupation, channel_sign)
        step = rows // slices
        return pl.pallas_call(
            exchange_kernel,
            grid=(slices,),
            out_shape=jax.ShapeDtypeStruct((1, rows, columns), jnp.float32),
            in_specs=[vmem, vmem, pl.BlockSpec((1, 1, columns), lambda m: (0, 0, 0))],
            out_specs=pl.BlockSpec((1, step, columns), lambda m: (0, m, 0)),
            compiler_params=pltpu.CompilerParams(vmem_limit_bytes=24 * 1024 * 1024),
        )(total, other, swap_perm)

    return jax.shard_map(
        shards,
        mesh=mesh,
        in_specs=(
            P("grp", "blk", None),
            P("grp", "blk", None),
            P("grp", "blk", None, None, None),
            P("grp", "blk", None),
            P("grp", "blk", None),
            P("grp", None),
            P(),
            P("grp", "blk", None),
        ),
        out_specs=P("grp", "blk", None),
        check_vma=False,
    )
```
